32 devices in a mesh: row: 4 (over z), col: 8 (over y, x, core).
Axes of the slice: x: 2, y: 2, z: 4, core: 2. Of those that a mesh axis runs over, the one named last changes fastest.
Arguments:
- out_grads: bfloat16 [8, 48, 28672], P('col', None, 'row'), may hold values from -6 to 6
- acts: bfloat16 [8, 48, 8192], P('row', None, 'col'), may hold values from -6 to 6
- rot_out: bfloat16 [28672, 28672], P('row', 'col'), may hold values from -0.03125 to 0.03125
- rot_in: bfloat16 [8192, 8192], P('col', 'row'), may hold values from -0.0625 to 0.0625
- queries: bfloat16 [2, 28672, 8192], P(None, 'col', 'row'), may hold values from -0.00036621094 to 0.00036621094
- token_sequence: int32 [256], replicated, may hold values from 0 to 7, never falling along the last dimension, each value on 1 to 48 neighbouring positions
Outputs:
- scores: float32 [256, 2], P(('row', 'col'))
The draws below stay inside these ranges and needn't reach their ends.
Inputs may be any that keep to these rules, and one draw needn't show every extreme that they name: `token_sequence`: values never fall along the tokens; every sequence 0 to 7 has 1 to 48 tokens, some sequence exactly 48; the k-th token of a sequence (from 0) sits in its slot k of out_grads and acts.
All inputs are finite; a program needn't handle non-finite values.
Results may differ from the reference program's by a relative error of at most 0.0041.
Values may be sent and summed in bfloat16 or wider, within the bound.
No kernel may reach another device: no remote copies, remote signals or barrier semaphores. Data moves between devices by JAX's collectives and lax.ppermute only.
A program may use at most 128 MiB of HBM per device.

```python
import math
import jax
import jax.numpy as jnp
import numpy as np

DIN = 8192
DOUT = 28672
NQ = 2
SLOTS = 48
SEQS = 8
TOKENS = 256


def level_of(rng, shape, split, low, high):
    gain = 1.0
    for axis_at, blocks in split:
        heights = jax.random.uniform(jax.random.fold_in(jax.random.fold_in(rng, 6), axis_at), (blocks,), jnp.float32, low / len(split), high / len(split))
        gain = gain * jnp.repeat(jnp.exp(heights), shape[axis_at] // blocks).reshape((-1,) + (1,) * (len(shape) - 1 - axis_at))
    return gain


def profile(count, total, bound, skew):
    weights = [(1 << 20) // math.isqrt(grade ** skew) + 1 for grade in range(2, count + 1)]
    rest, given = total - bound - (count - 1), [1] * (count - 1)
    while rest > 0:
        movable = [i for i in range(count - 1) if given[i] < bound]
        pool, left = sum([weights[i] for i in movable]), rest
        for i in movable:
            more = min(bound - given[i], max(1, left * weights[i] // pool), rest)
            given[i] = given[i] + more
            rest = rest - more
    return np.array([bound] + given)


def ragged_sizes(key, number_of, total, limit, skew):
    if number_of == 2:
        one = jax.random.randint(key, (), max(1, total - limit), min(limit, total - 1) + 1)
        return jnp.stack([one, total - one])
    lengths = jnp.asarray(profile(number_of, total, limit, skew), jnp.int32)
    couples = (number_of - 1) // 2
    giver, taker = lengths[1:1 + 2 * couples:2], lengths[2:2 + 2 * couples:2]
    room = jnp.minimum(giver - 1, limit - taker)
    shifted = jax.random.randint(jax.random.fold_in(key, 1), (couples,), 0, 1 << 20) % (room + 1)
    lengths = lengths.at[1:1 + 2 * couples:2].set(giver - shifted).at[2:2 + 2 * couples:2].set(taker + shifted)
    return lengths[jax.random.permutation(jax.random.fold_in(key, 2), number_of)]


def normal_values(key, dims, scale, reach, split=(), held_as=jnp.bfloat16):
    loudness = level_of(key, dims, split, -0.22, 0.18) if split else 1.0
    entries = jax.random.normal(key, dims, jnp.float32) * scale * loudness
    return jnp.minimum(jnp.maximum(entries, -reach), reach).astype(held_as)


def setup_inputs(seed: int = 0) -> dict:
    key_of = jax.random.split(jax.random.key(seed), 7)
    return {
        "out_grads": normal_values(key_of[0], (SEQS, SLOTS, DOUT), 1.0, 6.0, ((0, 8), (2, 4))),
        "acts": normal_values(key_of[1], (SEQS, SLOTS, DIN), 1.0, 6.0, ((0, 4), (2, 8))),
        "rot_out": normal_values(key_of[2], (DOUT, DOUT), DOUT ** -0.5, 0.03125, ((0, 4), (1, 8))),
        "rot_in": normal_values(key_of[3], (DIN, DIN), DIN ** -0.5, 0.0625, ((0, 8), (1, 4))),
        "queries": normal_values(key_of[4], (NQ, DOUT, DIN), (DOUT * DIN) ** -0.5, 0.00036621094, ((1, 8), (2, 4))),
        "token_sequence": jnp.searchsorted(jnp.cumsum(ragged_sizes(key_of[5], SEQS, TOKENS, SLOTS, 2)), jnp.arange(TOKENS), side="right").astype(jnp.int32),
    }


def token_places(token_sequence, seq_count, slot_count):
    token_count = token_sequence.shape[0]
    labels = jnp.arange(seq_count, dtype=jnp.int32)
    before = (token_sequence[:, None] < labels[None, :]).astype(jnp.int32)
    starts = jnp.sum(before, axis=0).astype(jnp.int32)
    member = (token_sequence[:, None] == labels[None, :]).astype(jnp.int32)
    own_start = jnp.sum(member * starts[None, :], axis=1).astype(jnp.int32)
    position = jnp.arange(token_count, dtype=jnp.int32) - own_start
    return (token_sequence * slot_count + position).astype(jnp.int32)


def reference(out_grads, acts, rot_out, rot_in, queries, token_sequence):
    flat_index = token_places(token_sequence, SEQS, SLOTS)
    grad_rows = out_grads.reshape(SEQS * SLOTS, DOUT)[flat_index]
    act_rows = acts.reshape(SEQS * SLOTS, DIN)[flat_index]
    rot_grads = jnp.dot(grad_rows, rot_out, preferred_element_type=jnp.float32).astype(jnp.bfloat16)
    rot_acts = jnp.dot(act_rows, rot_in, preferred_element_type=jnp.float32).astype(jnp.bfloat16)
    columns = []
    for query_index in range(NQ):
        projected = jnp.dot(rot_acts, queries[query_index].T, preferred_element_type=jnp.float32)
        columns.append(jnp.sum(rot_grads.astype(jnp.float32) * projected, axis=1))
    return jnp.stack(columns, axis=1)
```

```python
import jax
import jax.numpy as jnp
from jax import lax
from jax.experimental import pallas as pl
from jax.experimental.pallas import tpu as pltpu
from jax.sharding import PartitionSpec as P

F32 = jnp.float32
BF16 = jnp.bfloat16
LANES = 128
CHUNKS = 4


def block_of(size, limit):
    best = LANES
    for width in range(LANES, min(size, limit) + 1, LANES):
        if size % width == 0:
            best = width
    return best


def flip(value, axis, bit):
    return lax.ppermute(value, axis, [(i, i ^ bit) for i in range(lax.axis_size(axis))])


def token_places(token_sequence, seq_count):
    labels = jnp.arange(seq_count, dtype=jnp.int32)
    before = (token_sequence[:, None] < labels[None, :]).astype(jnp.int32)
    starts = jnp.sum(before, axis=0)
    member = (token_sequence[:, None] == labels[None, :]).astype(jnp.int32)
    own_start = jnp.sum(member * starts[None, :], axis=1)
    return jnp.arange(token_sequence.shape[0], dtype=jnp.int32) - own_start


def picker(shard_of, within, place, axis, shard_rows):
    column = (shard_of ^ lax.axis_index(axis)) * shard_rows + within + place
    width = lax.axis_size(axis) * shard_rows
    return (column[:, None] == jnp.arange(width, dtype=jnp.int32)[None, :]).astype(BF16)


def gather_half(own, axis, bits):
    have = {0: own}
    for bit in bits:
        for distance in list(have):
            have[distance ^ bit] = flip(have[distance], axis, bit)
    return have


def pack_rows(onehot, whole, first, second):
    tokens, slots_all = onehot.shape
    rows, features = whole[0].shape
    half = features // 2
    width = block_of(half, 1024)
    steps = half // width
    count = slots_all // rows
    keys_whole, keys_half = sorted(whole), sorted(first)

    def kernel(onehot_ref, *refs):
        out_ref = refs[-1]
        whole_refs = dict(zip(keys_whole, refs))
        first_refs = dict(zip(keys_half, refs[len(keys_whole):]))
        second_refs = dict(zip(keys_half, refs[len(keys_whole) + len(keys_half):]))

        def fill(half_refs):
            parts = [(whole_refs[k] if k in whole_refs else half_refs[k])[...] for k in range(count)]
            stacked = jnp.concatenate(parts, axis=0)
            out_ref[...] = jnp.dot(
                onehot_ref[...], stacked, preferred_element_type=F32
            ).astype(BF16)

        pl.when(pl.program_id(0) < steps)(lambda: fill(first_refs))
        pl.when(pl.program_id(0) >= steps)(lambda: fill(second_refs))

    shape = (rows, width)
    specs = [pl.BlockSpec((tokens, slots_all), lambda j: (0, 0))]
    specs += [pl.BlockSpec(shape, lambda j: (0, j)) for _ in keys_whole]
    specs += [pl.BlockSpec(shape, lambda j: (0, jnp.minimum(j, steps - 1))) for _ in keys_half]
    specs += [pl.BlockSpec(shape, lambda j: (0, jnp.maximum(j - steps, 0))) for _ in keys_half]
    return pl.pallas_call(
        kernel,
        grid=(2 * steps,),
        in_specs=specs,
        out_specs=pl.BlockSpec((tokens, width), lambda j: (0, j)),
        out_shape=jax.ShapeDtypeStruct((tokens, features), BF16),
        cost_estimate=pl.CostEstimate(
            flops=2 * tokens * slots_all * features,
            bytes_accessed=2 * features * (tokens + slots_all),
            transcendentals=0,
        ),
        name="pack_grads",
    )(
        onehot,
        *[whole[k] for k in keys_whole],
        *[first[k] for k in keys_half],
        *[second[k] for k in keys_half],
    )


def rotate_grads(rows, basis, start, width):
    tokens, depth = rows.shape
    deep = block_of(depth, 1024)
    steps = depth // deep
    unit = width
    while start % unit:
        unit -= LANES
    while width % unit or start % unit:
        unit -= LANES
    outs = width // unit

    def kernel(rows_ref, basis_ref, sum_ref, sent_ref):
        step = pl.program_id(1)
        part = jnp.dot(rows_ref[...], basis_ref[...], preferred_element_type=F32)

        @pl.when(step == 0)
        def _():
            sum_ref[...] = part

        @pl.when(step > 0)
        def _():
            sum_ref[...] += part

        @pl.when(step == steps - 1)
        def _():
            sent_ref[...] = sum_ref[...].astype(BF16)

    return pl.pallas_call(
        kernel,
        grid=(outs, steps),
        in_specs=[
            pl.BlockSpec((tokens, deep), lambda i, k: (0, k)),
            pl.BlockSpec((deep, unit), lambda i, k: (k, start // unit + i)),
        ],
        out_specs=[
            pl.BlockSpec((tokens, unit), lambda i, k: (0, i)),
            pl.BlockSpec((tokens, unit), lambda i, k: (0, i)),
        ],
        out_shape=[
            jax.ShapeDtypeStruct((tokens, width), F32),
            jax.ShapeDtypeStruct((tokens, width), BF16),
        ],
        cost_estimate=pl.CostEstimate(
            flops=2 * tokens * depth * width,
            bytes_accessed=2 * depth * (width + tokens) + 6 * tokens * width,
            transcendentals=0,
        ),
        name="rotate_grads",
    )(rows, basis)


def rotate_acts(onehot, blocks, basis):
    tokens, slots_all = onehot.shape
    depth, width = basis.shape
    unit = block_of(width, 512)

    def kernel(onehot_ref, *refs):
        basis_ref, out_ref, rows_ref = refs[-3:]

        @pl.when(pl.program_id(0) == 0)
        def _():
            stacked = jnp.concatenate([r[...] for r in refs[:-3]], axis=0)
            rows_ref[...] = jnp.dot(
                onehot_ref[...], stacked, preferred_element_type=F32
            ).astype(BF16)

        out_ref[...] = jnp.dot(rows_ref[...], basis_ref[...], preferred_element_type=F32)

    return pl.pallas_call(
        kernel,
        grid=(width // unit,),
        in_specs=[pl.BlockSpec((tokens, slots_all), lambda j: (0, 0))]
        + [pl.BlockSpec(b.shape, lambda j: (0, 0)) for b in blocks]
        + [pl.BlockSpec((depth, unit), lambda j: (0, j))],
        out_specs=pl.BlockSpec((tokens, unit), lambda j: (0, j)),
        out_shape=jax.ShapeDtypeStruct((tokens, width), F32),
        scratch_shapes=[pltpu.VMEM((tokens, depth), BF16)],
        cost_estimate=pl.CostEstimate(
            flops=2 * tokens * depth * (width + slots_all),
            bytes_accessed=2 * depth * (width + slots_all) + 4 * tokens * width,
            transcendentals=0,
        ),
        name="rotate_acts",
    )(onehot, *blocks, basis)


def project(acts_first, acts_second, queries):
    count, height, depth = queries.shape
    tokens, half = acts_first.shape
    unit = block_of(height, 512)
    contract = (((1,), (1,)), ((), ()))

    def kernel(first_ref, second_ref, queries_ref, out_ref):
        out_ref[0] = lax.dot_general(
            first_ref[...], queries_ref[0, :, :half], contract, preferred_element_type=F32
        ) + lax.dot_general(
            second_ref[...], queries_ref[0, :, half:], contract, preferred_element_type=F32
        )

    return pl.pallas_call(
        kernel,
        grid=(count, height // unit),
        in_specs=[
            pl.BlockSpec((tokens, half), lambda q, i: (0, 0)),
            pl.BlockSpec((tokens, depth - half), lambda q, i: (0, 0)),
            pl.BlockSpec((1, unit, depth), lambda q, i: (q, i, 0)),
        ],
        out_specs=pl.BlockSpec((1, tokens, unit), lambda q, i: (q, 0, i)),
        out_shape=jax.ShapeDtypeStruct((count, tokens, height), F32),
        cost_estimate=pl.CostEstimate(
            flops=2 * count * tokens * depth * height,
            bytes_accessed=count * height * (2 * depth + 4 * tokens),
            transcendentals=0,
        ),
        name="project",
    )(acts_first, acts_second, queries)


def index_bit(axis, bit):
    return (lax.axis_index(axis) // bit) % 2


def halve(total, axis, bit):
    high = index_bit(axis, bit)
    pair = total.reshape((2, total.shape[0] // 2) + total.shape[1:])
    sent = lax.dynamic_index_in_dim(pair, 1 - high, 0, keepdims=False)
    kept = lax.dynamic_index_in_dim(pair, high, 0, keepdims=False)
    return kept + flip(sent, axis, bit)


def unhalve(part, axis, bit):
    high = index_bit(axis, bit) == 1
    other = flip(part, axis, bit)
    return jnp.concatenate([jnp.where(high, other, part), jnp.where(high, part, other)], axis=0)


def sum_acts(part, axis):
    bits = [1 << b for b in range(lax.axis_size(axis).bit_length() - 1)]
    near, far = bits[:1], bits[1:]
    for bit in near:
        part = halve(part, axis, bit)
    half = part.shape[1] // 2
    done = []
    pieces = [part[:, :half], part[:, half:]]
    orders = [far, far[::-1]]
    for stage in range(len(far)):
        pieces = [halve(p, axis, o[stage]) for p, o in zip(pieces, orders)]
    pieces = [p.astype(BF16) for p in pieces]
    for stage in reversed(range(len(far))):
        pieces = [unhalve(p, axis, o[stage]) for p, o in zip(pieces, orders)]
    for bit in near:
        pieces = [unhalve(p, axis, bit) for p in pieces]
    return pieces


def sum_line(total, sent, axis):
    count = lax.axis_size(axis)
    middle = count // 2
    for s in range(middle - 1):
        got = lax.ppermute(sent, axis, [(s, s + 1), (count - 1 - s, count - 2 - s)])
        total = total + got.astype(F32)
        sent = total.astype(BF16)
    got = lax.ppermute(sent, axis, [(middle - 1, middle), (middle, middle - 1)])
    total = total + got.astype(F32)
    sent = total.astype(BF16)
    place = lax.axis_index(axis)
    for s in reversed(range(middle - 1)):
        got = lax.ppermute(sent, axis, [(s + 1, s), (count - 2 - s, count - 1 - s)])
        takes = (place == s) | (place == count - 1 - s)
        total = jnp.where(takes, got.astype(F32), total)
        sent = jnp.where(takes, got, sent)
    return total


def chunks_of(size, count):
    units = size // LANES
    edges = [units * i // count * LANES for i in range(count)] + [size]
    return [(a, b - a) for a, b in zip(edges, edges[1:]) if b > a]


def local(out_grads, acts, rot_out, rot_in, queries, token_sequence):
    tokens = token_sequence.shape[0]
    rows, cols = lax.axis_size("row"), lax.axis_size("col")
    seqs, slots, features = out_grads.shape
    act_seqs = acts.shape[0]
    place = token_places(token_sequence, seqs * cols)
    grad_pick = picker(
        token_sequence // seqs, (token_sequence % seqs) * slots, place, "col", seqs * slots
    )
    act_pick = picker(
        token_sequence // act_seqs, (token_sequence % act_seqs) * slots, place, "row", act_seqs * slots
    )

    own = out_grads.reshape(seqs * slots, features)
    half = features // 2
    far = [1 << b for b in range(1, cols.bit_length() - 1)]
    first = gather_half(own[:, :half], "col", far)
    second = gather_half(own[:, half:], "col", far[::-1])
    whole = {0: own, 1: flip(own, "col", 1)}
    for near in (first, second):
        del near[0]
        for distance in list(near):
            near[distance ^ 1] = flip(near[distance], "col", 1)

    held = [acts.reshape(act_seqs * slots, acts.shape[2])]
    for b in range(rows.bit_length() - 1):
        held = held + [flip(h, "row", 1 << b) for h in held]
    act_sums = rotate_acts(act_pick, held, rot_in)

    packed = pack_rows(grad_pick, whole, first, second)

    totals = []
    for start, width in chunks_of(rot_out.shape[1], CHUNKS):
        total, sent = rotate_grads(packed, rot_out, start, width)
        totals.append((start, width, sum_line(total, sent, "row")))

    rot_acts = sum_acts(act_sums, "col")
    projected = project(*rot_acts, queries)
    scores = 0.0
    for start, width, total in totals:
        scores = scores + jnp.sum(projected[:, :, start : start + width] * total[None], axis=2)

    count = scores.shape[0]
    shards = rows * cols
    spread = scores.reshape(count, shards, tokens // shards).transpose(1, 0, 2)
    spread = spread.reshape(shards, count * tokens // shards)
    spread = lax.all_to_all(spread, ("row", "col"), 0, 0, tiled=True)
    return jnp.sum(spread, axis=0).reshape(count, tokens // shards).T


def solution(mesh):
    placed = (
        P("col", None, "row"),
        P("row", None, "col"),
        P("row", "col"),
        P("col", "row"),
        P(None, "col", "row"),
        P(),
    )
    return jax.shard_map(
        local, mesh=mesh, in_specs=placed, out_specs=P(("row", "col"), None), check_vma=False
    )
```

```python
import jax
import jax.numpy as jnp
from jax import lax
from jax.experimental import pallas as pl
from jax.experimental.pallas import tpu as pltpu
from jax.sharding import PartitionSpec as P

F32 = jnp.float32
BF16 = jnp.bfloat16
LANES = 128
WIDE = 512
CHUNKS = 4


def block_of(size, limit):
    best = LANES
    for width in range(LANES, min(size, limit) + 1, LANES):
        if size % width == 0:
            best = width
    return best


def limit(need):
    return pltpu.CompilerParams(vmem_limit_bytes=max(need + (6 << 20), 24 << 20))


class Column:
    def __init__(self, axis):
        self.axis = axis
        self.count = lax.axis_size(axis)
        self.stages = max(self.count.bit_length() - 2, 0)
        self.index = lax.axis_index(axis)

    def near(self, value):
        return lax.ppermute(value, self.axis, [(i, i ^ 1) for i in range(self.count)])

    def far(self, value, stage):
        def partner(i):
            return i ^ (2 << (stage if i % 2 == 0 else self.stages - 1 - stage))

        return lax.ppermute(value, self.axis, [(i, partner(i)) for i in range(self.count)])

    def reverse(self, value):
        out = jnp.zeros_like(value)
        for b in range(self.stages):
            out = out | (((value >> b) & 1) << (self.stages - 1 - b))
        return out

    def arrival(self, source):
        apart = source ^ self.index
        links = apart >> 1
        stage_bits = jnp.where((source & 1) == 0, links, self.reverse(links))
        return ((apart & 1) << self.stages) + stage_bits

    def place(self, target):
        apart = target ^ self.index
        links = apart >> 1
        stage_bits = jnp.where((target & 1) == 0, self.reverse(links), links)
        return ((apart & 1) << self.stages) + stage_bits

    def gather(self, own):
        have = [own]
        far = []
        for s in range(self.stages):
            far.append([self.far(own, s)])
        for s in range(self.stages):
            far[s] = far[s] + [self.far(block, s) for block in have[1:]]
            have = have + far[s]
        out = []
        for block in have:
            out.append(self.near(block))
        return have + out

    def reduce(self, low, high):
        part = low + self.near(high)
        for s in range(self.stages):
            half = part.shape[0] // 2
            part = part[:half] + self.far(part[half:], s)
        return part

    def spread(self, part):
        for s in reversed(range(self.stages)):
            part = jnp.concatenate([part, self.far(part, s)], axis=0)
        return jnp.concatenate([part, self.near(part)], axis=0)


def token_slots(token_sequence, seq_count):
    labels = jnp.arange(seq_count, dtype=jnp.int32)
    before = (token_sequence[:, None] < labels[None, :]).astype(jnp.int32)
    starts = jnp.sum(before, axis=0)
    member = (token_sequence[:, None] == labels[None, :]).astype(jnp.int32)
    own_start = jnp.sum(member * starts[None, :], axis=1)
    return jnp.arange(token_sequence.shape[0], dtype=jnp.int32) - own_start


def one_hot(index, width):
    return (index[:, None] == jnp.arange(width, dtype=jnp.int32)[None, :]).astype(BF16)


def fetch(sources, target, sems):
    copies, at = [], 0
    for k, source in enumerate(sources):
        rows = source.shape[0]
        copies.append(pltpu.make_async_copy(source, target.at[pl.ds(at, rows)], sems.at[k]))
        copies[-1].start()
        at += rows
    return copies


def in_hbm(values):
    return [pltpu.with_memory_space_constraint(v, pltpu.HBM) for v in values]


HBM = pl.BlockSpec(memory_space=pltpu.HBM)
VMEM = pl.BlockSpec(memory_space=pltpu.VMEM)


def pack_rows(onehot, blocks):
    tokens, slots_all = onehot.shape
    features = blocks[0].shape[1]
    width = block_of(features, 1792)
    parts = features // width

    def kernel(onehot_ref, *refs):
        sources, (out_ref, rows_ref, sems) = refs[:-3], refs[-3:]
        copies = []

        def start(p):
            columns = pl.ds(p * width, width)
            copies.append(
                fetch([r.at[:, columns] for r in sources], rows_ref.at[:, columns], sems.at[p])
            )

        start(0)
        for p in range(parts):
            if p + 1 < parts:
                start(p + 1)
            for copy in copies[p]:
                copy.wait()
            columns = pl.ds(p * width, width)
            out_ref[:, columns] = jnp.dot(
                onehot_ref[...], rows_ref[:, columns], preferred_element_type=F32
            ).astype(BF16)

    return pl.pallas_call(
        kernel,
        in_specs=[VMEM] + [HBM] * len(blocks),
        out_specs=VMEM,
        out_shape=jax.ShapeDtypeStruct((tokens, features), BF16),
        scratch_shapes=[
            pltpu.VMEM((slots_all, features), BF16),
            pltpu.SemaphoreType.DMA((parts, len(blocks))),
        ],
        compiler_params=limit(2 * (tokens * slots_all + (slots_all + 2 * tokens) * features)),
        cost_estimate=pl.CostEstimate(
            flops=2 * tokens * slots_all * features,
            bytes_accessed=2 * features * (tokens + slots_all),
            transcendentals=0,
        ),
        name="pack_grads",
    )(onehot, *in_hbm(blocks))


def rotate_grads(rows, basis, start, width):
    tokens, depth = rows.shape
    unit = block_of(width, WIDE)
    deep = block_of(depth, 1792)
    pieces = [(i, k) for i in range(width // unit) for k in range(depth // deep)]
    ahead = min(4, len(pieces))

    def kernel(rows_ref, basis_ref, sum_ref, sent_ref, held_ref, sems):
        def copy(n):
            i, k = pieces[n]
            return pltpu.make_async_copy(
                basis_ref.at[pl.ds(k * deep, deep), pl.ds(start + i * unit, unit)],
                held_ref.at[n % (ahead + 1)],
                sems.at[n % (ahead + 1)],
            )

        for n in range(ahead):
            copy(n).start()
        for n, (i, k) in enumerate(pieces):
            if n + ahead < len(pieces):
                copy(n + ahead).start()
            copy(n).wait()
            part = jnp.dot(
                rows_ref[:, pl.ds(k * deep, deep)],
                held_ref[n % (ahead + 1)],
                preferred_element_type=F32,
            )
            columns = pl.ds(i * unit, unit)
            if k > 0:
                part = sum_ref[:, columns] + part
            sum_ref[:, columns] = part
            if k == depth // deep - 1:
                sent_ref[:, columns] = part.astype(BF16)

    return pl.pallas_call(
        kernel,
        in_specs=[VMEM, HBM],
        out_specs=[VMEM, VMEM],
        out_shape=[
            jax.ShapeDtypeStruct((tokens, width), F32),
            jax.ShapeDtypeStruct((tokens, width), BF16),
        ],
        scratch_shapes=[
            pltpu.VMEM((ahead + 1, deep, unit), BF16),
            pltpu.SemaphoreType.DMA((ahead + 1,)),
        ],
        compiler_params=limit(2 * (ahead + 1) * deep * unit + 2 * tokens * (depth + 4 * width)),
        cost_estimate=pl.CostEstimate(
            flops=2 * tokens * depth * width,
            bytes_accessed=2 * depth * (width + tokens) + 6 * tokens * width,
            transcendentals=0,
        ),
        name="rotate_grads",
    )(rows, *in_hbm([basis]))


def rotate_acts(onehot, blocks, basis):
    tokens, slots_all = onehot.shape
    depth, width = basis.shape
    unit = block_of(width, WIDE)
    half = tokens // 2

    def kernel(onehot_ref, *refs):
        sources = refs[:-5]
        basis_ref, low_ref, high_ref, held_ref, sems = refs[-5:]
        copies = []
        for k, at in enumerate(range(0, width, unit)):
            columns = pl.ds(at, unit)
            copies.append(
                pltpu.make_async_copy(basis_ref.at[:, columns], held_ref.at[:, columns], sems.at[k])
            )
            copies[k].start()
        slots = jnp.concatenate([r[...] for r in sources], axis=0)
        rows = jnp.dot(onehot_ref[...], slots, preferred_element_type=F32).astype(BF16)
        for k, at in enumerate(range(0, width, unit)):
            columns = pl.ds(at, unit)
            copies[k].wait()
            part = jnp.dot(rows, held_ref[:, columns], preferred_element_type=F32)
            low_ref[:, columns] = part[:half]
            high_ref[:, columns] = part[half:]

    shape = jax.ShapeDtypeStruct((half, width), F32)
    return pl.pallas_call(
        kernel,
        in_specs=[VMEM] * (len(blocks) + 1) + [HBM],
        out_specs=[VMEM, VMEM],
        out_shape=[shape, shape],
        scratch_shapes=[
            pltpu.VMEM((depth, width), BF16),
            pltpu.SemaphoreType.DMA((width // unit,)),
        ],
        compiler_params=limit(
            2 * (tokens * slots_all + (2 * slots_all + width + 3 * tokens) * depth) + 6 * tokens * width
        ),
        cost_estimate=pl.CostEstimate(
            flops=2 * tokens * depth * (width + slots_all),
            bytes_accessed=2 * depth * (width + slots_all) + 4 * tokens * width,
            transcendentals=0,
        ),
        name="rotate_acts",
    )(onehot, *blocks, *in_hbm([basis]))


def project(rot_acts, queries, start, width):
    count, _, depth = queries.shape
    tokens = rot_acts.shape[0]
    unit = block_of(width, WIDE)
    pieces = [(q, i) for q in range(count) for i in range(width // unit)]
    ahead = min(3, len(pieces))

    def kernel(acts_ref, queries_ref, out_ref, held_ref, sems):
        def copy(n):
            q, i = pieces[n]
            return pltpu.make_async_copy(
                queries_ref.at[q, pl.ds(start + i * unit, unit)],
                held_ref.at[n % (ahead + 1)],
                sems.at[n % (ahead + 1)],
            )

        for n in range(ahead):
            copy(n).start()
        for n, (q, i) in enumerate(pieces):
            if n + ahead < len(pieces):
                copy(n + ahead).start()
            copy(n).wait()
            out_ref[q, :, pl.ds(i * unit, unit)] = lax.dot_general(
                acts_ref[...],
                held_ref[n % (ahead + 1)],
                (((1,), (1,)), ((), ())),
                preferred_element_type=F32,
            )

    return pl.pallas_call(
        kernel,
        in_specs=[VMEM, HBM],
        out_specs=VMEM,
        out_shape=jax.ShapeDtypeStruct((count, tokens, width), F32),
        scratch_shapes=[
            pltpu.VMEM((ahead + 1, unit, depth), BF16),
            pltpu.SemaphoreType.DMA((ahead + 1,)),
        ],
        compiler_params=limit(
            2 * depth * (tokens + (ahead + 1) * unit) + 4 * tokens * (count * width + unit)
        ),
        cost_estimate=pl.CostEstimate(
            flops=2 * count * tokens * depth * width,
            bytes_accessed=count * width * (2 * depth + 4 * tokens),
            transcendentals=0,
        ),
        name="project",
    )(rot_acts, *in_hbm([queries]))


def score(inner, own, inward, outward, projected):
    count, tokens, width = projected.shape
    unit = block_of(width, WIDE)

    def kernel(inner_ref, own_ref, *refs):
        outward_ref, projected_ref, out_ref = refs[-3:]

        @pl.when(pl.program_id(0) == 0)
        def _():
            out_ref[...] = jnp.zeros_like(out_ref)

        def add(total):
            for q in range(count):
                terms = projected_ref[q] * total
                part = terms[:, :LANES]
                for k in range(LANES, unit, LANES):
                    part = part + terms[:, k : k + LANES]
                out_ref[q] += part

        @pl.when(inner_ref[0] == 1)
        def _():
            total = own_ref[...]
            for r in refs[:-3]:
                total = total + r[...].astype(F32)
            add(total)

        @pl.when(inner_ref[0] == 0)
        def _():
            add(outward_ref[...].astype(F32))

    block = pl.BlockSpec((tokens, unit), lambda j: (0, j))
    return pl.pallas_call(
        kernel,
        grid=(width // unit,),
        in_specs=[pl.BlockSpec(memory_space=pltpu.SMEM)]
        + [block] * (len(inward) + 2)
        + [pl.BlockSpec((count, tokens, unit), lambda j: (0, 0, j))],
        out_specs=pl.BlockSpec((count, tokens, LANES), lambda j: (0, 0, 0)),
        out_shape=jax.ShapeDtypeStruct((count, tokens, LANES), F32),
        compiler_params=limit(2 * tokens * unit * (8 * count + 8 + 2 * len(inward))),
        cost_estimate=pl.CostEstimate(
            flops=2 * count * tokens * width,
            bytes_accessed=tokens * width * (4 * count + 6 + 2 * len(inward)),
            transcendentals=0,
        ),
        name="score",
    )(inner, own, *inward, outward, projected)


def line_steps(count):
    middle = count // 2
    inward = [[(s, s + 1), (count - 1 - s, count - 2 - s)] for s in range(middle - 1)]
    across = [(middle - 1, middle), (middle, middle - 1)]
    outward = [[(b, a) for a, b in pairs] for pairs in reversed(inward)]
    return inward + [across], outward


def chunks_of(size, count):
    unit = WIDE if size % WIDE == 0 else LANES
    units = size // unit
    most = -(-units // count)
    edges = [min(most * i, units) * unit for i in range(count + 1)]
    return [(a, b - a) for a, b in zip(edges, edges[1:]) if b > a]


def program(out_grads, acts, rot_out, rot_in, queries, token_sequence):
    tokens = token_sequence.shape[0]
    rows = lax.axis_size("row")
    col = Column("col")
    cols = col.count
    seqs, slots, features = out_grads.shape
    act_seqs = acts.shape[0]
    share = tokens // (rows * cols)

    held = [acts.reshape(act_seqs * slots, acts.shape[2])]
    for apart in range(1, rows):
        held.append(lax.ppermute(held[0], "row", [(i, i ^ apart) for i in range(rows)]))
    grads = col.gather(out_grads.reshape(seqs * slots, features))

    place = col.place(jnp.arange(cols, dtype=jnp.int32))
    order = place[:, None] == jnp.arange(cols, dtype=jnp.int32)[None, :]
    slot = token_slots(token_sequence, seqs * cols)
    grad_source = col.arrival(token_sequence // seqs) * seqs + token_sequence % seqs
    act_source = ((token_sequence // act_seqs) ^ lax.axis_index("row")) * act_seqs
    act_source = act_source + token_sequence % act_seqs

    def in_order(index):
        index = index.reshape(rows, cols, 1, share)
        index = jnp.where(order.reshape(1, cols, cols, 1), index, 0).sum(axis=1)
        return index.transpose(1, 0, 2).reshape(tokens)

    grad_pick = one_hot(in_order(grad_source * slots + slot), cols * seqs * slots)
    act_pick = one_hot(in_order(act_source * slots + slot), rows * act_seqs * slots)

    low, high = rotate_acts(act_pick, held, rot_in)
    packed = pack_rows(grad_pick, grads)

    inward, outward = line_steps(rows)
    chunks = []
    for start, width in chunks_of(rot_out.shape[1], CHUNKS):
        own, sent = rotate_grads(packed, rot_out, start, width)
        total, gots = own, []
        for pairs in inward:
            gots.append(lax.ppermute(sent, "row", pairs))
            total = total + gots[-1].astype(F32)
            sent = total.astype(BF16)
        chunks.append((start, width, own, gots, sent))

    rot_acts = col.spread(col.reduce(low, high).astype(BF16))

    z = lax.axis_index("row")
    inner = ((z == rows // 2 - 1) | (z == rows // 2)).astype(jnp.int32).reshape(1)
    scores = 0.0
    for start, width, own, gots, sent in chunks:
        projected = project(rot_acts, queries, start, width)
        back = sent
        for step, pairs in enumerate(outward):
            got = lax.ppermute(sent, "row", pairs)
            taken = (z == pairs[0][1]) | (z == pairs[1][1])
            back = got if step == 0 else jnp.where(taken, got, back)
            sent = back
        scores = scores + score(inner, own, gots, back, projected)

    count = scores.shape[0]
    scores = jnp.sum(scores, axis=2).reshape(count, 1, cols, rows, share)
    scores = jnp.sum(jnp.where(order.reshape(1, cols, cols, 1, 1), scores, 0.0), axis=2)
    spread = scores.transpose(2, 1, 0, 3).reshape(rows * cols, count * share)
    spread = lax.all_to_all(spread, ("row", "col"), 0, 0, tiled=True)
    return jnp.sum(spread, axis=0).reshape(count, share).T


def solution(mesh):
    placed = (
        P("col", None, "row"),
        P("row", None, "col"),
        P("row", "col"),
        P("col", "row"),
        P(None, "col", "row"),
        P(),
    )
    return jax.shard_map(
        program, mesh=mesh, in_specs=placed, out_specs=P(("row", "col"), None), check_vma=False
    )
```

```python
import jax
import jax.numpy as jnp
from jax import lax
from jax.experimental import pallas as pl
from jax.experimental.pallas import tpu as pltpu
from jax.sharding import PartitionSpec as P

F32 = jnp.float32
BF16 = jnp.bfloat16
LANES = 128
WIDE = 512
PARTS = (2, 2, 2, 1)


def block_of(size, limit):
    best = LANES
    for width in range(LANES, min(size, limit) + 1, LANES):
        if size % width == 0:
            best = width
    return best


def limit(need):
    return pltpu.CompilerParams(vmem_limit_bytes=max(need + (6 << 20), 24 << 20))


class Column:
    def __init__(self, axis):
        self.axis = axis
        self.count = lax.axis_size(axis)
        self.stages = max(self.count.bit_length() - 2, 0)
        self.index = lax.axis_index(axis)

    def near(self, value):
        return lax.ppermute(value, self.axis, [(i, i ^ 1) for i in range(self.count)])

    def far(self, value, stage):
        def partner(i):
            return i ^ (2 << (stage if i % 2 == 0 else self.stages - 1 - stage))

        return lax.ppermute(value, self.axis, [(i, partner(i)) for i in range(self.count)])

    def reverse(self, value):
        out = jnp.zeros_like(value)
        for b in range(self.stages):
            out = out | (((value >> b) & 1) << (self.stages - 1 - b))
        return out

    def arrival(self, source):
        apart = source ^ self.index
        links = apart >> 1
        stage_bits = jnp.where((source & 1) == 0, links, self.reverse(links))
        return ((apart & 1) << self.stages) + stage_bits

    def place(self, target):
        apart = target ^ self.index
        links = apart >> 1
        stage_bits = jnp.where((target & 1) == 0, self.reverse(links), links)
        return ((apart & 1) << self.stages) + stage_bits

    def gather(self, own):
        have = [own]
        far = []
        for s in range(self.stages):
            far.append([self.far(own, s)])
        for s in range(self.stages):
            far[s] = far[s] + [self.far(block, s) for block in have[1:]]
            have = have + far[s]
        out = []
        for block in have:
            out.append(self.near(block))
        return have + out

    def reduce(self, low, high):
        part = low + self.near(high)
        for s in range(self.stages):
            half = part.shape[0] // 2
            part = part[:half] + self.far(part[half:], s)
        return part

    def spread(self, part):
        for s in reversed(range(self.stages)):
            part = jnp.concatenate([part, self.far(part, s)], axis=0)
        return jnp.concatenate([part, self.near(part)], axis=0)


def token_slots(token_sequence, seq_count):
    labels = jnp.arange(seq_count, dtype=jnp.int32)
    before = (token_sequence[:, None] < labels[None, :]).astype(jnp.int32)
    starts = jnp.sum(before, axis=0)
    member = (token_sequence[:, None] == labels[None, :]).astype(jnp.int32)
    own_start = jnp.sum(member * starts[None, :], axis=1)
    return jnp.arange(token_sequence.shape[0], dtype=jnp.int32) - own_start


def one_hot(index, width):
    return (index[:, None] == jnp.arange(width, dtype=jnp.int32)[None, :]).astype(BF16)


def fetch(sources, target, sems):
    copies, at = [], 0
    for k, source in enumerate(sources):
        rows = source.shape[0]
        copies.append(pltpu.make_async_copy(source, target.at[pl.ds(at, rows)], sems.at[k]))
        copies[-1].start()
        at += rows
    return copies


def in_hbm(values):
    return [pltpu.with_memory_space_constraint(v, pltpu.HBM) for v in values]


HBM = pl.BlockSpec(memory_space=pltpu.HBM)
VMEM = pl.BlockSpec(memory_space=pltpu.VMEM)


def pack_rows(onehot, blocks):
    tokens, slots_all = onehot.shape
    features = blocks[0].shape[1]
    width = block_of(features, 1792)
    parts = features // width

    def kernel(onehot_ref, *refs):
        sources, (out_ref, rows_ref, sems) = refs[:-3], refs[-3:]
        copies = []

        def start(p):
            columns = pl.ds(p * width, width)
            copies.append(
                fetch([r.at[:, columns] for r in sources], rows_ref.at[:, columns], sems.at[p])
            )

        start(0)
        for p in range(parts):
            if p + 1 < parts:
                start(p + 1)
            for copy in copies[p]:
                copy.wait()
            columns = pl.ds(p * width, width)
            out_ref[:, columns] = jnp.dot(
                onehot_ref[...], rows_ref[:, columns], preferred_element_type=F32
            ).astype(BF16)

    return pl.pallas_call(
        kernel,
        in_specs=[VMEM] + [HBM] * len(blocks),
        out_specs=VMEM,
        out_shape=jax.ShapeDtypeStruct((tokens, features), BF16),
        scratch_shapes=[
            pltpu.VMEM((slots_all, features), BF16),
            pltpu.SemaphoreType.DMA((parts, len(blocks))),
        ],
        compiler_params=limit(2 * (tokens * slots_all + (slots_all + 2 * tokens) * features)),
        cost_estimate=pl.CostEstimate(
            flops=2 * tokens * slots_all * features,
            bytes_accessed=2 * features * (tokens + slots_all),
            transcendentals=0,
        ),
        name="pack_grads",
    )(onehot, *in_hbm(blocks))


def rotate_grads(rows, basis, start, width):
    tokens, depth = rows.shape
    unit = block_of(width, WIDE)
    deep = block_of(depth, 1792)
    pieces = [(i, k) for i in range(width // unit) for k in range(depth // deep)]
    ahead = min(4, len(pieces))

    def kernel(rows_ref, basis_ref, sum_ref, sent_ref, held_ref, sems):
        def copy(n):
            i, k = pieces[n]
            return pltpu.make_async_copy(
                basis_ref.at[pl.ds(k * deep, deep), pl.ds(start + i * unit, unit)],
                held_ref.at[n % (ahead + 1)],
                sems.at[n % (ahead + 1)],
            )

        for n in range(ahead):
            copy(n).start()
        for n, (i, k) in enumerate(pieces):
            if n + ahead < len(pieces):
                copy(n + ahead).start()
            copy(n).wait()
            part = jnp.dot(
                rows_ref[:, pl.ds(k * deep, deep)],
                held_ref[n % (ahead + 1)],
                preferred_element_type=F32,
            )
            columns = pl.ds(i * unit, unit)
            if k > 0:
                part = sum_ref[:, columns] + part
            sum_ref[:, columns] = part
            if k == depth // deep - 1:
                sent_ref[:, columns] = part.astype(BF16)

    return pl.pallas_call(
        kernel,
        in_specs=[VMEM, HBM],
        out_specs=[VMEM, VMEM],
        out_shape=[
            jax.ShapeDtypeStruct((tokens, width), F32),
            jax.ShapeDtypeStruct((tokens, width), BF16),
        ],
        scratch_shapes=[
            pltpu.VMEM((ahead + 1, deep, unit), BF16),
            pltpu.SemaphoreType.DMA((ahead + 1,)),
        ],
        compiler_params=limit(2 * (ahead + 1) * deep * unit + 2 * tokens * (depth + 4 * width)),
        cost_estimate=pl.CostEstimate(
            flops=2 * tokens * depth * width,
            bytes_accessed=2 * depth * (width + tokens) + 6 * tokens * width,
            transcendentals=0,
        ),
        name="rotate_grads",
    )(rows, *in_hbm([basis]))


def rotate_acts(onehot, blocks, basis):
    tokens, slots_all = onehot.shape
    depth, width = basis.shape
    unit = block_of(width, WIDE)
    half = tokens // 2

    def kernel(onehot_ref, *refs):
        sources = refs[:-5]
        basis_ref, low_ref, high_ref, held_ref, sems = refs[-5:]
        copies = []
        for k, at in enumerate(range(0, width, unit)):
            columns = pl.ds(at, unit)
            copies.append(
                pltpu.make_async_copy(basis_ref.at[:, columns], held_ref.at[:, columns], sems.at[k])
            )
            copies[k].start()
        slots = jnp.concatenate([r[...] for r in sources], axis=0)
        rows = jnp.dot(onehot_ref[...], slots, preferred_element_type=F32).astype(BF16)
        for k, at in enumerate(range(0, width, unit)):
            columns = pl.ds(at, unit)
            copies[k].wait()
            part = jnp.dot(rows, held_ref[:, columns], preferred_element_type=F32)
            low_ref[:, columns] = part[:half]
            high_ref[:, columns] = part[half:]

    shape = jax.ShapeDtypeStruct((half, width), F32)
    return pl.pallas_call(
        kernel,
        in_specs=[VMEM] * (len(blocks) + 1) + [HBM],
        out_specs=[VMEM, VMEM],
        out_shape=[shape, shape],
        scratch_shapes=[
            pltpu.VMEM((depth, width), BF16),
            pltpu.SemaphoreType.DMA((width // unit,)),
        ],
        compiler_params=limit(
            2 * (tokens * slots_all + (2 * slots_all + width + 3 * tokens) * depth) + 6 * tokens * width
        ),
        cost_estimate=pl.CostEstimate(
            flops=2 * tokens * depth * (width + slots_all),
            bytes_accessed=2 * depth * (width + slots_all) + 4 * tokens * width,
            transcendentals=0,
        ),
        name="rotate_acts",
    )(onehot, *blocks, *in_hbm([basis]))


def project(rot_acts, queries, start, width):
    count, _, depth = queries.shape
    tokens = rot_acts.shape[0]
    unit = block_of(width, WIDE)
    pieces = [(q, i) for q in range(count) for i in range(width // unit)]
    ahead = min(3, len(pieces))

    def kernel(acts_ref, queries_ref, out_ref, held_ref, sems):
        def copy(n):
            q, i = pieces[n]
            return pltpu.make_async_copy(
                queries_ref.at[q, pl.ds(start + i * unit, unit)],
                held_ref.at[n % (ahead + 1)],
                sems.at[n % (ahead + 1)],
            )

        for n in range(ahead):
            copy(n).start()
        for n, (q, i) in enumerate(pieces):
            if n + ahead < len(pieces):
                copy(n + ahead).start()
            copy(n).wait()
            out_ref[q, :, pl.ds(i * unit, unit)] = lax.dot_general(
                acts_ref[...],
                held_ref[n % (ahead + 1)],
                (((1,), (1,)), ((), ())),
                preferred_element_type=F32,
            )

    return pl.pallas_call(
        kernel,
        in_specs=[VMEM, HBM],
        out_specs=VMEM,
        out_shape=jax.ShapeDtypeStruct((count, tokens, width), F32),
        scratch_shapes=[
            pltpu.VMEM((ahead + 1, unit, depth), BF16),
            pltpu.SemaphoreType.DMA((ahead + 1,)),
        ],
        compiler_params=limit(
            2 * depth * (tokens + (ahead + 1) * unit) + 4 * tokens * (count * width + unit)
        ),
        cost_estimate=pl.CostEstimate(
            flops=2 * count * tokens * depth * width,
            bytes_accessed=count * width * (2 * depth + 4 * tokens),
            transcendentals=0,
        ),
        name="project",
    )(rot_acts, *in_hbm([queries]))


def score(inner, kept, outward, projected):
    count, tokens, width = projected.shape
    unit = block_of(width, WIDE)

    def kernel(inner_ref, kept_ref, outward_ref, projected_ref, out_ref):
        def add(total_ref):
            parts = [None] * count
            for at in range(0, width, unit):
                total = total_ref[:, pl.ds(at, unit)].astype(F32)
                for q in range(count):
                    terms = projected_ref[q, :, pl.ds(at, unit)] * total
                    for k in range(0, unit, LANES):
                        term = terms[:, k : k + LANES]
                        parts[q] = term if parts[q] is None else parts[q] + term
            for q in range(count):
                out_ref[q] = parts[q]

        pl.when(inner_ref[0] == 1)(lambda: add(kept_ref))
        pl.when(inner_ref[0] == 0)(lambda: add(outward_ref))

    return pl.pallas_call(
        kernel,
        in_specs=[pl.BlockSpec(memory_space=pltpu.SMEM)] + [VMEM] * 3,
        out_specs=VMEM,
        out_shape=jax.ShapeDtypeStruct((count, tokens, LANES), F32),
        compiler_params=limit(tokens * (width * (4 * count + 4) + 8 * count * LANES + 8 * unit)),
        cost_estimate=pl.CostEstimate(
            flops=2 * count * tokens * width,
            bytes_accessed=tokens * width * (4 * count + 4),
            transcendentals=0,
        ),
        name="score",
    )(inner, kept, outward, projected)


def line_steps(count):
    middle = count // 2
    inward = [[(s, s + 1), (count - 1 - s, count - 2 - s)] for s in range(middle - 1)]
    across = [(middle - 1, middle), (middle, middle - 1)]
    outward = [[(b, a) for a, b in pairs] for pairs in reversed(inward)]
    return inward + [across], outward


def chunks_of(size):
    unit = WIDE if size % WIDE == 0 else LANES
    units = size // unit
    edges = [sum(PARTS[:k]) * units // sum(PARTS) * unit for k in range(len(PARTS) + 1)]
    return [(a, b - a) for a, b in zip(edges, edges[1:])]


def program(out_grads, acts, rot_out, rot_in, queries, token_sequence):
    tokens = token_sequence.shape[0]
    rows = lax.axis_size("row")
    col = Column("col")
    cols = col.count
    seqs, slots, features = out_grads.shape
    act_seqs = acts.shape[0]
    share = tokens // (rows * cols)

    held = [acts.reshape(act_seqs * slots, acts.shape[2])]
    for apart in range(1, rows):
        held.append(lax.ppermute(held[0], "row", [(i, i ^ apart) for i in range(rows)]))
    grads = col.gather(out_grads.reshape(seqs * slots, features))

    place = col.place(jnp.arange(cols, dtype=jnp.int32))
    order = place[:, None] == jnp.arange(cols, dtype=jnp.int32)[None, :]
    slot = token_slots(token_sequence, seqs * cols)
    grad_source = col.arrival(token_sequence // seqs) * seqs + token_sequence % seqs
    act_source = ((token_sequence // act_seqs) ^ lax.axis_index("row")) * act_seqs
    act_source = act_source + token_sequence % act_seqs

    def in_order(index):
        index = index.reshape(rows, cols, 1, share)
        index = jnp.where(order.reshape(1, cols, cols, 1), index, 0).sum(axis=1)
        return index.transpose(1, 0, 2).reshape(tokens)

    grad_pick = one_hot(in_order(grad_source * slots + slot), cols * seqs * slots)
    act_pick = one_hot(in_order(act_source * slots + slot), rows * act_seqs * slots)

    low, high = rotate_acts(act_pick, held, rot_in)
    packed = pack_rows(grad_pick, grads)

    inward, outward = line_steps(rows)
    chunks = []
    for start, width in chunks_of(rot_out.shape[1]):
        own, sent = rotate_grads(packed, rot_out, start, width)
        total = own
        for pairs in inward:
            total = total + lax.ppermute(sent, "row", pairs).astype(F32)
            sent = total.astype(BF16)
        chunks.append((start, width, sent))

    rot_acts = col.spread(col.reduce(low, high).astype(BF16))

    z = lax.axis_index("row")
    inner = ((z == rows // 2 - 1) | (z == rows // 2)).astype(jnp.int32).reshape(1)
    scores = 0.0
    for start, width, sent in chunks:
        projected = project(rot_acts, queries, start, width)
        kept = back = sent
        for step, pairs in enumerate(outward):
            got = lax.ppermute(sent, "row", pairs)
            taken = (z == pairs[0][1]) | (z == pairs[1][1])
            back = got if step == 0 else jnp.where(taken, got, back)
            sent = back
        scores = scores + score(inner, kept, back, projected)

    count = scores.shape[0]
    scores = jnp.sum(scores, axis=2).reshape(count, 1, cols, rows, share)
    scores = jnp.sum(jnp.where(order.reshape(1, cols, cols, 1, 1), scores, 0.0), axis=2)
    spread = scores.transpose(2, 1, 0, 3).reshape(rows * cols, count * share)
    spread = lax.all_to_all(spread, ("row", "col"), 0, 0, tiled=True)
    return jnp.sum(spread, axis=0).reshape(count, share).T


def solution(mesh):
    placed = (
        P("col", None, "row"),
        P("row", None, "col"),
        P("row", "col"),
        P("col", "row"),
        P(None, "col", "row"),
        P(),
    )
    return jax.shard_map(
        program, mesh=mesh, in_specs=placed, out_specs=P(("row", "col"), None), check_vma=False
    )
```

```python
import jax
import jax.numpy as jnp
from jax import lax
from jax.experimental import pallas as pl
from jax.experimental.pallas import tpu as pltpu
from jax.sharding import PartitionSpec as P

F32 = jnp.float32
BF16 = jnp.bfloat16
LANES = 128
WIDE = 512
PARTS = (2, 2, 2, 1)


def block_of(size, limit):
    best = LANES
    for width in range(LANES, min(size, limit) + 1, LANES):
        if size % width == 0:
            best = width
    return best


def limit(need):
    return pltpu.CompilerParams(vmem_limit_bytes=max(need + (6 << 20), 24 << 20))


class Column:
    def __init__(self, axis):
        self.axis = axis
        self.count = lax.axis_size(axis)
        self.stages = max(self.count.bit_length() - 2, 0)
        self.index = lax.axis_index(axis)

    def near(self, value):
        return lax.ppermute(value, self.axis, [(i, i ^ 1) for i in range(self.count)])

    def far(self, value, stage):
        def partner(i):
            return i ^ (2 << (stage if i % 2 == 0 else self.stages - 1 - stage))

        return lax.ppermute(value, self.axis, [(i, partner(i)) for i in range(self.count)])

    def reverse(self, value):
        out = jnp.zeros_like(value)
        for b in range(self.stages):
            out = out | (((value >> b) & 1) << (self.stages - 1 - b))
        return out

    def arrival(self, source):
        apart = source ^ self.index
        links = apart >> 1
        stage_bits = jnp.where((source & 1) == 0, links, self.reverse(links))
        return ((apart & 1) << self.stages) + stage_bits

    def place(self, target):
        apart = target ^ self.index
        links = apart >> 1
        stage_bits = jnp.where((target & 1) == 0, self.reverse(links), links)
        return ((apart & 1) << self.stages) + stage_bits

    def gather(self, own):
        have = [own]
        far = []
        for s in range(self.stages):
            far.append([self.far(own, s)])
        for s in range(self.stages):
            far[s] = far[s] + [self.far(block, s) for block in have[1:]]
            have = have + far[s]
        out = []
        for block in have:
            out.append(self.near(block))
        return have + out

    def reduce(self, low, high):
        part = low + self.near(high)
        for s in range(self.stages):
            half = part.shape[0] // 2
            part = part[:half] + self.far(part[half:], s)
        return part

    def spread(self, part):
        for s in reversed(range(self.stages)):
            part = jnp.concatenate([part, self.far(part, s)], axis=0)
        return jnp.concatenate([part, self.near(part)], axis=0)


def token_slots(token_sequence, seq_count):
    labels = jnp.arange(seq_count, dtype=jnp.int32)
    before = (token_sequence[:, None] < labels[None, :]).astype(jnp.int32)
    starts = jnp.sum(before, axis=0)
    member = (token_sequence[:, None] == labels[None, :]).astype(jnp.int32)
    own_start = jnp.sum(member * starts[None, :], axis=1)
    return jnp.arange(token_sequence.shape[0], dtype=jnp.int32) - own_start


def one_hot(index, width):
    return (index[:, None] == jnp.arange(width, dtype=jnp.int32)[None, :]).astype(BF16)


def fetch(sources, target, sems):
    copies, at = [], 0
    for k, source in enumerate(sources):
        rows = source.shape[0]
        copies.append(pltpu.make_async_copy(source, target.at[pl.ds(at, rows)], sems.at[k]))
        copies[-1].start()
        at += rows
    return copies


def in_hbm(values):
    return [pltpu.with_memory_space_constraint(v, pltpu.HBM) for v in values]


HBM = pl.BlockSpec(memory_space=pltpu.HBM)
VMEM = pl.BlockSpec(memory_space=pltpu.VMEM)


def pack_rows(onehot, blocks):
    tokens, slots_all = onehot.shape
    features = blocks[0].shape[1]
    width = block_of(features, 1792)
    parts = features // width

    def kernel(onehot_ref, *refs):
        sources, (out_ref, rows_ref, sems) = refs[:-3], refs[-3:]
        copies = []

        def start(p):
            columns = pl.ds(p * width, width)
            copies.append(
                fetch([r.at[:, columns] for r in sources], rows_ref.at[:, columns], sems.at[p])
            )

        for p in range(parts):
            start(p)
        for p in range(parts):
            for copy in copies[p]:
                copy.wait()
            columns = pl.ds(p * width, width)
            out_ref[:, columns] = jnp.dot(
                onehot_ref[...], rows_ref[:, columns], preferred_element_type=F32
            ).astype(BF16)

    return pl.pallas_call(
        kernel,
        in_specs=[VMEM] + [HBM] * len(blocks),
        out_specs=VMEM,
        out_shape=jax.ShapeDtypeStruct((tokens, features), BF16),
        scratch_shapes=[
            pltpu.VMEM((slots_all, features), BF16),
            pltpu.SemaphoreType.DMA((parts, len(blocks))),
        ],
        compiler_params=limit(2 * (tokens * slots_all + (slots_all + 2 * tokens) * features)),
        cost_estimate=pl.CostEstimate(
            flops=2 * tokens * slots_all * features,
            bytes_accessed=2 * features * (tokens + slots_all),
            transcendentals=0,
        ),
        name="pack_grads",
    )(onehot, *in_hbm(blocks))


def rotate_grads(rows, basis, start, width):
    tokens, depth = rows.shape
    unit = block_of(width, WIDE)
    deep = block_of(depth, 1792)
    pieces = [(i, k) for i in range(width // unit) for k in range(depth // deep)]
    ahead = min(4, len(pieces))

    def kernel(rows_ref, basis_ref, sum_ref, sent_ref, held_ref, sems):
        def copy(n):
            i, k = pieces[n]
            return pltpu.make_async_copy(
                basis_ref.at[pl.ds(k * deep, deep), pl.ds(start + i * unit, unit)],
                held_ref.at[n % (ahead + 1)],
                sems.at[n % (ahead + 1)],
            )

        for n in range(ahead):
            copy(n).start()
        for n, (i, k) in enumerate(pieces):
            if n + ahead < len(pieces):
                copy(n + ahead).start()
            copy(n).wait()
            part = jnp.dot(
                rows_ref[:, pl.ds(k * deep, deep)],
                held_ref[n % (ahead + 1)],
                preferred_element_type=F32,
            )
            columns = pl.ds(i * unit, unit)
            if k > 0:
                part = sum_ref[:, columns] + part
            sum_ref[:, columns] = part
            if k == depth // deep - 1:
                sent_ref[:, columns] = part.astype(BF16)

    return pl.pallas_call(
        kernel,
        in_specs=[VMEM, HBM],
        out_specs=[VMEM, VMEM],
        out_shape=[
            jax.ShapeDtypeStruct((tokens, width), F32),
            jax.ShapeDtypeStruct((tokens, width), BF16),
        ],
        scratch_shapes=[
            pltpu.VMEM((ahead + 1, deep, unit), BF16),
            pltpu.SemaphoreType.DMA((ahead + 1,)),
        ],
        compiler_params=limit(2 * (ahead + 1) * deep * unit + 2 * tokens * (depth + 4 * width)),
        cost_estimate=pl.CostEstimate(
            flops=2 * tokens * depth * width,
            bytes_accessed=2 * depth * (width + tokens) + 6 * tokens * width,
            transcendentals=0,
        ),
        name="rotate_grads",
    )(rows, *in_hbm([basis]))


def rotate_acts(onehot, blocks, basis):
    tokens, slots_all = onehot.shape
    depth, width = basis.shape
    unit = block_of(width, WIDE)
    half = tokens // 2

    def kernel(onehot_ref, *refs):
        sources = refs[:-5]
        basis_ref, low_ref, high_ref, held_ref, sems = refs[-5:]
        copies = []
        for k, at in enumerate(range(0, width, unit)):
            columns = pl.ds(at, unit)
            copies.append(
                pltpu.make_async_copy(basis_ref.at[:, columns], held_ref.at[:, columns], sems.at[k])
            )
            copies[k].start()
        slots = jnp.concatenate([r[...] for r in sources], axis=0)
        rows = jnp.dot(onehot_ref[...], slots, preferred_element_type=F32).astype(BF16)
        for k, at in enumerate(range(0, width, unit)):
            columns = pl.ds(at, unit)
            copies[k].wait()
            part = jnp.dot(rows, held_ref[:, columns], preferred_element_type=F32)
            low_ref[:, columns] = part[:half]
            high_ref[:, columns] = part[half:]

    shape = jax.ShapeDtypeStruct((half, width), F32)
    return pl.pallas_call(
        kernel,
        in_specs=[VMEM] * (len(blocks) + 1) + [HBM],
        out_specs=[VMEM, VMEM],
        out_shape=[shape, shape],
        scratch_shapes=[
            pltpu.VMEM((depth, width), BF16),
            pltpu.SemaphoreType.DMA((width // unit,)),
        ],
        compiler_params=limit(
            2 * (tokens * slots_all + (2 * slots_all + width + 3 * tokens) * depth) + 6 * tokens * width
        ),
        cost_estimate=pl.CostEstimate(
            flops=2 * tokens * depth * (width + slots_all),
            bytes_accessed=2 * depth * (width + slots_all) + 4 * tokens * width,
            transcendentals=0,
        ),
        name="rotate_acts",
    )(onehot, *blocks, *in_hbm([basis]))


def project(rot_acts, queries, start, width):
    count, _, depth = queries.shape
    tokens = rot_acts.shape[0]
    unit = block_of(width, WIDE)
    pieces = [(q, i) for q in range(count) for i in range(width // unit)]
    ahead = min(3, len(pieces))

    def kernel(acts_ref, queries_ref, out_ref, held_ref, sems):
        def copy(n):
            q, i = pieces[n]
            return pltpu.make_async_copy(
                queries_ref.at[q, pl.ds(start + i * unit, unit)],
                held_ref.at[n % (ahead + 1)],
                sems.at[n % (ahead + 1)],
            )

        for n in range(ahead):
            copy(n).start()
        for n, (q, i) in enumerate(pieces):
            if n + ahead < len(pieces):
                copy(n + ahead).start()
            copy(n).wait()
            out_ref[q, :, pl.ds(i * unit, unit)] = lax.dot_general(
                acts_ref[...],
                held_ref[n % (ahead + 1)],
                (((1,), (1,)), ((), ())),
                preferred_element_type=F32,
            )

    return pl.pallas_call(
        kernel,
        in_specs=[VMEM, HBM],
        out_specs=VMEM,
        out_shape=jax.ShapeDtypeStruct((count, tokens, width), F32),
        scratch_shapes=[
            pltpu.VMEM((ahead + 1, unit, depth), BF16),
            pltpu.SemaphoreType.DMA((ahead + 1,)),
        ],
        compiler_params=limit(
            2 * depth * (tokens + (ahead + 1) * unit) + 4 * tokens * (count * width + unit)
        ),
        cost_estimate=pl.CostEstimate(
            flops=2 * count * tokens * depth * width,
            bytes_accessed=count * width * (2 * depth + 4 * tokens),
            transcendentals=0,
        ),
        name="project",
    )(rot_acts, *in_hbm([queries]))


def score(inner, kept, outward, projected):
    count, tokens, width = projected.shape
    unit = block_of(width, WIDE)

    def kernel(inner_ref, kept_ref, *refs):
        projected_ref, out_ref = refs[-2:]

        def add(total_ref):
            parts = [None] * count
            for at in range(0, width, unit):
                total = total_ref[:, pl.ds(at, unit)].astype(F32)
                for q in range(count):
                    terms = projected_ref[q, :, pl.ds(at, unit)] * total
                    for k in range(0, unit, LANES):
                        term = terms[:, k : k + LANES]
                        parts[q] = term if parts[q] is None else parts[q] + term
            for q in range(count):
                out_ref[q] = parts[q]

        pl.when(inner_ref[0] == 1)(lambda: add(kept_ref))

        @pl.when(inner_ref[0] == 0)
        def _():
            if outward is None:
                out_ref[...] = jnp.zeros_like(out_ref)
            else:
                add(refs[0])

    return pl.pallas_call(
        kernel,
        in_specs=[pl.BlockSpec(memory_space=pltpu.SMEM)] + [VMEM] * (2 if outward is None else 3),
        out_specs=VMEM,
        out_shape=jax.ShapeDtypeStruct((count, tokens, LANES), F32),
        compiler_params=limit(tokens * (width * (4 * count + 4) + 8 * count * LANES + 8 * unit)),
        cost_estimate=pl.CostEstimate(
            flops=2 * count * tokens * width,
            bytes_accessed=tokens * width * (4 * count + 4),
            transcendentals=0,
        ),
        name="score",
    )(inner, kept, *([] if outward is None else [outward]), projected)


def line_steps(count):
    middle = count // 2
    inward = [[(s, s + 1), (count - 1 - s, count - 2 - s)] for s in range(middle - 1)]
    across = [(middle - 1, middle), (middle, middle - 1)]
    outward = [[(b, a) for a, b in pairs] for pairs in reversed(inward)]
    return inward + [across], outward


def chunks_of(size):
    unit = WIDE if size % WIDE == 0 else LANES
    units = size // unit
    edges = [sum(PARTS[:k]) * units // sum(PARTS) * unit for k in range(len(PARTS) + 1)]
    return [(a, b - a) for a, b in zip(edges, edges[1:])]


def program(out_grads, acts, rot_out, rot_in, queries, token_sequence):
    tokens = token_sequence.shape[0]
    rows = lax.axis_size("row")
    col = Column("col")
    cols = col.count
    seqs, slots, features = out_grads.shape
    act_seqs = acts.shape[0]
    share = tokens // (rows * cols)

    held = [acts.reshape(act_seqs * slots, acts.shape[2])]
    for apart in range(1, rows):
        held.append(lax.ppermute(held[0], "row", [(i, i ^ apart) for i in range(rows)]))
    grads = col.gather(out_grads.reshape(seqs * slots, features))

    place = col.place(jnp.arange(cols, dtype=jnp.int32))
    order = place[:, None] == jnp.arange(cols, dtype=jnp.int32)[None, :]
    slot = token_slots(token_sequence, seqs * cols)
    grad_source = col.arrival(token_sequence // seqs) * seqs + token_sequence % seqs
    act_source = ((token_sequence // act_seqs) ^ lax.axis_index("row")) * act_seqs
    act_source = act_source + token_sequence % act_seqs

    def in_order(index):
        index = index.reshape(rows, cols, 1, share)
        index = jnp.where(order.reshape(1, cols, cols, 1), index, 0).sum(axis=1)
        return index.transpose(1, 0, 2).reshape(tokens)

    grad_pick = one_hot(in_order(grad_source * slots + slot), cols * seqs * slots)
    act_pick = one_hot(in_order(act_source * slots + slot), rows * act_seqs * slots)

    low, high = rotate_acts(act_pick, held, rot_in)
    packed = pack_rows(grad_pick, grads)

    inward, outward = line_steps(rows)
    chunks = []
    for start, width in chunks_of(rot_out.shape[1]):
        own, sent = rotate_grads(packed, rot_out, start, width)
        total = own
        for pairs in inward:
            total = total + lax.ppermute(sent, "row", pairs).astype(F32)
            sent = total.astype(BF16)
        chunks.append((start, width, sent))

    rot_acts = col.spread(col.reduce(low, high).astype(BF16))

    z = lax.axis_index("row")
    inner = ((z == rows // 2 - 1) | (z == rows // 2)).astype(jnp.int32).reshape(1)
    last = len(chunks) - 1
    scores = 0.0
    for k, (start, width, sent) in enumerate(chunks):
        projected = project(rot_acts, queries, start, width)
        kept = back = sent
        if k == last:
            for pairs in inward[:-1]:
                got = lax.ppermute(projected.astype(BF16), "row", pairs)
                projected = projected + got.astype(F32)
            back = None
        else:
            for step, pairs in enumerate(outward):
                got = lax.ppermute(sent, "row", pairs)
                taken = (z == pairs[0][1]) | (z == pairs[1][1])
                back = got if step == 0 else jnp.where(taken, got, back)
                sent = back
        scores = scores + score(inner, kept, back, projected)

    count = scores.shape[0]
    scores = jnp.sum(scores, axis=2).reshape(count, 1, cols, rows, share)
    scores = jnp.sum(jnp.where(order.reshape(1, cols, cols, 1, 1), scores, 0.0), axis=2)
    spread = scores.transpose(2, 1, 0, 3).reshape(rows * cols, count * share)
    spread = lax.all_to_all(spread, ("row", "col"), 0, 0, tiled=True)
    return jnp.sum(spread, axis=0).reshape(count, share).T


def solution(mesh):
    placed = (
        P("col", None, "row"),
        P("row", None, "col"),
        P("row", "col"),
        P("col", "row"),
        P(None, "col", "row"),
        P(),
    )
    return jax.shard_map(
        program, mesh=mesh, in_specs=placed, out_specs=P(("row", "col"), None), check_vma=False
    )
```
